256 devices in a mesh: freq: 32 (over x, y, core), node: 8 (over z).
Axes of the slice: x: 4, y: 4, z: 8, core: 2. Of those that a mesh axis runs over, the one named last changes fastest.
Arguments:
- pressure: bfloat16 [2, 128, 4, 65536], P(None, 'freq', None, 'node'), may hold values from -6 to 6
- spectrum_amp: float32 [4, 128], replicated, may hold values from 0.03 to 0.3
- phase_code: int32 [4, 128], replicated, may hold values from 0 to 4095
- panel_tile: int32 [32, 8, 256, 1], P('freq'), may hold values from 0 to 255; in each aligned block of 2048 rows (0 to 2047, 2048 to 4095, ..., all dimensions but the last counted through in order) at most 12 rows name the same one
- patch_weight: bfloat16 [32, 8, 256, 128], P('freq'), may hold values from 0 to 0.099609375
Outputs:
- node_loads: bfloat16 [4, 4096, 32768], P(None, 'node', 'freq')
The draws below stay inside these ranges and needn't reach their ends.
Inputs may be any that keep to these rules, and one draw needn't show every extreme that they name: Within each block panel_tile[g] (2048 panels), no patch is named by more than 12 panels, a bound that some block reaches; every patch is named somewhere.
All inputs are finite; a program needn't handle non-finite values.
Results may differ from the reference program's by a relative error of at most 0.0062.
Values may be sent and summed in bfloat16 or wider, within the bound.
No kernel may reach another device: no remote copies, remote signals or barrier semaphores. Data moves between devices by JAX's collectives and lax.ppermute only.
A program may use at most 128 MiB of HBM per device.

```python
import math
import jax
import jax.numpy as jnp
import numpy as np
from jax import lax

F = 128
H = 4
TSTEPS = 4096
BIN_STEP = 15
PHASE_LEVELS = 4096
PAN_DEV = 256
PANELS = 65536
TILES = 256
NODES = 32768
CAPT = 12
N_FREQ = 32
N_NODE = 8


def place_ends(array, rng, least, largest):
    longest = array.shape.index(max(array.shape))
    spots = []
    for shift in (0, 1):
        where = [jax.random.randint(jax.random.fold_in(rng, axis), (), 0, length) for axis, length in enumerate(array.shape)]
        where[longest] = (where[longest] + shift) % array.shape[longest]
        spots.append(tuple(where))
    return array.at[spots[0]].set(least).at[spots[1]].set(largest)


def steps_of(stream_key, extent, split, least, largest):
    level = 1.0
    for axis_at, blocks in split:
        steps = jax.random.uniform(jax.random.fold_in(jax.random.fold_in(stream_key, 6), axis_at), (blocks,), jnp.float32, least / len(split), largest / len(split))
        level = level * jnp.repeat(jnp.exp(steps), extent[axis_at] // blocks).reshape((-1,) + (1,) * (len(extent) - 1 - axis_at))
    return level


def deal_out(rng, own, number, rows, number_of, top, reach, skew):
    ranking = jax.random.permutation(rng, number_of)
    packed, usual = load_shares(number_of, rows * top, reach, skew, True), load_shares(number_of, rows * top, reach, skew, False)
    places = jnp.arange(number_of)

    def named(tallies, rotation):
        used = int((tallies > 0).sum())
        fixed = max(1, used // 4)
        shifted = fixed + (places - fixed + rotation * (used - fixed)) % max(1, number_of - fixed)
        return jnp.zeros((number_of,), jnp.int32).at[ranking[jnp.where(places < fixed, places, shifted)]].set(jnp.asarray(tallies, jnp.int32))

    tallies = jnp.where(number % 4 == 0, named(packed, number // 4), named(usual, number - number // 4 - 1))
    mixed = jax.random.permutation(jax.random.fold_in(own, 3), number_of)
    giver, taker = mixed[0:number_of // 2 * 2:2], mixed[1:number_of // 2 * 2:2]
    room = jnp.minimum(tallies[giver] - 1, reach - tallies[taker]) // 2
    room = jnp.where((giver == ranking[0]) | (taker == ranking[0]) | (tallies[taker] == 0), 0, jnp.maximum(room, 0))
    shifted = jax.random.randint(jax.random.fold_in(own, 4), (number_of // 2,), 0, 1 << 20) % (room + 1)
    tallies = tallies.at[giver].add(-shifted).at[taker].add(shifted)
    labels = jnp.searchsorted(jnp.cumsum(tallies), jnp.arange(rows * top), side="right").astype(jnp.int32)
    grid = labels.reshape(top, rows).T
    grid = grid[jax.random.permutation(jax.random.fold_in(own, 1), rows)]
    rotation = jax.random.randint(jax.random.fold_in(own, 2), (rows, 1), 0, top)
    return jnp.take_along_axis(grid, (jnp.arange(top)[None, :] + rotation) % top, axis=1)


def load_shares(amount, total, reach, skew, full):
    loads = [(1 << 20) // math.isqrt(grade ** skew) + 1 for grade in range(1, amount + 1)]
    largest = reach if full else min(reach, max(-(-total // amount), total * loads[0] // sum(loads)))
    least = 1 if total - largest >= amount - 1 else 0
    given, rest = [largest] + [least] * (amount - 1), total - largest - least * (amount - 1)
    while rest > 0:
        movable = [i for i in range(1, amount) if given[i] < largest] or [i for i in range(1, amount) if given[i] < reach]
        whole, remaining = sum([loads[i] for i in movable]), rest
        for i in movable:
            extra = min(reach - given[i], max(1, remaining * loads[i] // whole), rest)
            given[i] = given[i] + extra
            rest = rest - extra
    return np.array(given)


def centred(key, extent, deviation, limit, pieces=(), held_as=jnp.bfloat16):
    gain = steps_of(key, extent, pieces, -0.22, 0.18) if pieces else 1.0
    array = jax.random.normal(key, extent, jnp.float32) * deviation * gain
    return jnp.minimum(jnp.maximum(array, -limit), limit).astype(held_as)


def setup_inputs(seed: int = 0) -> dict:
    key_list = jax.random.split(jax.random.key(seed), 6)
    pressure = centred(key_list[0], (2, F, H, PANELS), 1.0, 6.0, ((1, 32), (3, 8)))
    spectrum_amp = jnp.clip(jnp.exp(jax.random.uniform(key_list[1], (H, F), jnp.float32, math.log(0.03), math.log(0.3))), 0.03, 0.3)
    phase_code = place_ends(jax.random.randint(key_list[2], (H, F), 0, PHASE_LEVELS), jax.random.fold_in(key_list[2], 1), 0, PHASE_LEVELS - 1).astype(jnp.int32)
    panel_tile_keys = jax.random.split(jax.random.fold_in(key_list[3], 1), N_FREQ * N_NODE * PAN_DEV // (N_NODE * PAN_DEV))
    panel_tile_turns = jax.random.permutation(jax.random.fold_in(key_list[3], 3), N_FREQ * N_NODE * PAN_DEV // (N_NODE * PAN_DEV))
    panel_tile = jax.vmap(lambda own, number: deal_out(jax.random.fold_in(key_list[3], 2), own, number, N_NODE * PAN_DEV, TILES, 1, CAPT, 1))(panel_tile_keys, panel_tile_turns).reshape((N_FREQ, N_NODE, PAN_DEV, 1))
    patch_weight = jnp.clip(0.099609375 * jax.random.uniform(key_list[4], (N_FREQ, N_NODE, PAN_DEV, 128), jnp.float32) ** steps_of(key_list[4], (N_FREQ, N_NODE, PAN_DEV, 128), ((0, 32),), -0.2, 0.2), 0.0, 0.099609375).astype(jnp.bfloat16)
    return {"pressure": pressure, "spectrum_amp": spectrum_amp, "phase_code": phase_code, "panel_tile": panel_tile, "patch_weight": patch_weight}


def scale_spectra(pressure, spectrum_amp, phase_code):
    phase_angle = phase_code.astype(jnp.float32) * (2.0 * math.pi / PHASE_LEVELS)
    amplitude = spectrum_amp.T[:, :, None]
    cosine = jnp.cos(phase_angle).T[:, :, None]
    sine_part = jnp.sin(phase_angle).T[:, :, None]
    real_part = pressure[0].astype(jnp.float32)
    imag_part = pressure[1].astype(jnp.float32)
    scaled_re = amplitude * (real_part * cosine - imag_part * sine_part)
    scaled_im = amplitude * (real_part * sine_part + imag_part * cosine)
    return jnp.stack([scaled_re, scaled_im]).astype(jnp.bfloat16)


def basis_table(first_step, step_count):
    freq_bin = 1 + BIN_STEP * jnp.arange(F, dtype=jnp.int32)
    step_ids = first_step + jnp.arange(step_count, dtype=jnp.int32)
    turn_count = (freq_bin[:, None] * step_ids[None, :]) % TSTEPS
    turn_angle = turn_count.astype(jnp.float32) * (2.0 * math.pi / TSTEPS)
    return jnp.concatenate([jnp.cos(turn_angle), -jnp.sin(turn_angle)], axis=0).astype(jnp.bfloat16)


def reference(pressure, spectrum_amp, phase_code, panel_tile, patch_weight):
    scaled = scale_spectra(pressure, spectrum_amp, phase_code)
    flat_spectra = scaled.reshape(2 * F, H, PANELS).astype(jnp.float32)
    tile_ids = jnp.transpose(panel_tile, (1, 0, 2, 3)).reshape(PANELS).astype(jnp.int32)
    weights = jnp.transpose(patch_weight, (1, 0, 2, 3)).reshape(PANELS, 128)
    per_tile = N_FREQ * CAPT
    onehot = (tile_ids[:, None] == jnp.arange(TILES, dtype=jnp.int32)[None, :]).astype(jnp.int32)
    slot_rank = jnp.sum((jnp.cumsum(onehot, axis=0) - onehot) * onehot, axis=1)
    slot_index = tile_ids * per_tile + slot_rank
    members = jnp.full((TILES * per_tile,), PANELS, jnp.int32).at[slot_index].set(jnp.arange(PANELS, dtype=jnp.int32))
    tile_weight = jnp.take(weights, members, axis=0, mode="fill", fill_value=0)
    tile_weight = tile_weight.reshape(TILES, per_tile, 128).astype(jnp.float32)
    block_len = math.gcd(TSTEPS, 128)

    def one_block(block_index):
        wave_basis = basis_table(block_index * block_len, block_len).astype(jnp.float32)
        series = jnp.einsum('khp,kt->pht', flat_spectra, wave_basis).astype(jnp.bfloat16)
        gathered = jnp.take(series.reshape(PANELS, H * block_len), members, axis=0, mode="fill", fill_value=0)
        gathered = gathered.reshape(TILES, per_tile, H * block_len).astype(jnp.float32)
        partial_value = jnp.einsum('bsr,bsn->rbn', gathered, tile_weight)
        return partial_value.reshape(H, block_len, NODES).astype(jnp.bfloat16)

    block_loads = lax.map(one_block, jnp.arange(TSTEPS // block_len, dtype=jnp.int32))
    return jnp.transpose(block_loads, (1, 0, 2, 3)).reshape(H, TSTEPS, NODES)
```

```python
import math

import jax
import jax.numpy as jnp
from jax import lax
from jax.experimental import pallas as pl
from jax.experimental.pallas import tpu as pltpu
from jax.sharding import PartitionSpec as P

F = 128
TSTEPS = 4096
BIN_STEP = 15
PHASE_LEVELS = 4096
TILE_DEV = 8
BF = jnp.bfloat16
F32 = jnp.float32


def scale_kernel(group_ref, pressure_ref, amp_ref, code_ref, out_ref):
    owners, width = out_ref.shape[0], out_ref.shape[3]
    fl_count = pressure_ref.shape[1]
    lane = lax.broadcasted_iota(jnp.int32, amp_ref.shape, 1)
    angle = code_ref[...].astype(F32) * (2.0 * math.pi / PHASE_LEVELS)
    cosine, sine = jnp.cos(angle), jnp.sin(angle)
    amp = amp_ref[...]
    for fl in range(fl_count):
        chosen = lane == group_ref[0] * fl_count + fl

        def pick(table):
            return jnp.sum(jnp.where(chosen, table, 0.0), axis=1, keepdims=True)

        a, c, s = pick(amp), pick(cosine), pick(sine)

        for g in range(owners):
            cols = pl.ds(g * width, width)
            re = pressure_ref[0, fl, :, cols].astype(F32)
            im = pressure_ref[1, fl, :, cols].astype(F32)
            out_ref[g, fl] = (a * (re * c - im * s)).astype(BF)
            out_ref[g, fl_count + fl] = (a * (re * s + im * c)).astype(BF)


def scale_spectra(pressure, spectrum_amp, phase_code, group, owners):
    parts, fl_count, headings, panels = pressure.shape
    width = panels // owners
    return pl.pallas_call(
        scale_kernel,
        out_shape=jax.ShapeDtypeStruct((owners, parts * fl_count, headings, width), BF),
        in_specs=[
            pl.BlockSpec(memory_space=pltpu.SMEM),
            pl.BlockSpec(memory_space=pltpu.VMEM),
            pl.BlockSpec(memory_space=pltpu.VMEM),
            pl.BlockSpec(memory_space=pltpu.VMEM),
        ],
        out_specs=pl.BlockSpec(memory_space=pltpu.VMEM),
        cost_estimate=pl.CostEstimate(flops=2_000_000, bytes_accessed=1 << 20, transcendentals=0),
        name="scale",
    )(group.reshape(1), pressure, spectrum_amp, phase_code)


def fill_tilehot(tile_ref, hot_ref, tile_count):
    blocks, width = tile_ref.shape
    tile_iota = lax.broadcasted_iota(jnp.int32, (tile_count, width), 0)
    for k in range(blocks):
        hot = tile_iota == tile_ref[k : k + 1, :]
        hot_ref[:, k * width : (k + 1) * width] = jnp.where(hot, 1.0, 0.0).astype(BF)


def gather_slots(hot_ref, rank_ref, source_ref, out_ref, transposed):
    blocks, width = rank_ref.shape
    owners, capacity, tiles, lanes = out_ref.shape

    def one(s, carry):
        total = jnp.zeros((owners * tiles, lanes), F32)
        for k in range(blocks):
            cols = slice(k * width, (k + 1) * width)
            live = jnp.where(rank_ref[k : k + 1, :] == s.astype(F32), 1.0, 0.0).astype(BF)
            picked = hot_ref[:, cols] * live
            if transposed:
                total += lax.dot_general(
                    picked, source_ref[:, cols], (((1,), (1,)), ((), ())),
                    preferred_element_type=F32,
                )
            else:
                total += jnp.dot(picked, source_ref[cols, :], preferred_element_type=F32)
        out_ref[:, pl.ds(s, 1)] = total.astype(BF).reshape(owners, 1, tiles, lanes)
        return carry

    lax.fori_loop(0, capacity, one, 0)


def weight_kernel(tile_ref, weight_ref, out_ref, rank_ref, hot_ref):
    owners, _, tiles, _ = out_ref.shape
    blocks, width = tile_ref.shape
    fill_tilehot(tile_ref, hot_ref, owners * tiles)
    before = (
        lax.broadcasted_iota(jnp.int32, (width, width), 0)
        < lax.broadcasted_iota(jnp.int32, (width, width), 1)
    )
    before = jnp.where(before, 1.0, 0.0).astype(BF)
    seen = jnp.zeros((owners * tiles, 1), F32)
    for k in range(blocks):
        hot = hot_ref[:, k * width : (k + 1) * width]
        hot32 = hot.astype(F32)
        earlier = jnp.dot(hot, before, preferred_element_type=F32) + seen
        rank_ref[k : k + 1, :] = jnp.sum(hot32 * earlier, axis=0, keepdims=True)
        seen = seen + jnp.sum(hot32, axis=1, keepdims=True)
    gather_slots(hot_ref, rank_ref, weight_ref, out_ref, False)


def gather_weights(tile_ids, weights, owners, capacity):
    blocks, width = tile_ids.shape
    lanes = weights.shape[1]
    return pl.pallas_call(
        weight_kernel,
        out_shape=(
            jax.ShapeDtypeStruct((owners, capacity, TILE_DEV, lanes), BF),
            jax.ShapeDtypeStruct((blocks, width), F32),
        ),
        in_specs=[pl.BlockSpec(memory_space=pltpu.VMEM)] * 2,
        out_specs=(pl.BlockSpec(memory_space=pltpu.VMEM),) * 2,
        scratch_shapes=[pltpu.VMEM((owners * TILE_DEV, blocks * width), BF)],
        cost_estimate=pl.CostEstimate(
            flops=2 * owners * capacity * TILE_DEV * blocks * width * lanes,
            bytes_accessed=2 << 20, transcendentals=0,
        ),
        name="weight_slots",
    )(tile_ids, weights)


def row_kernel(tile_ref, rank_ref, spectra_ref, out_ref, hot_ref, rows_ref, packed_ref):
    groups, blocks, headings, width = spectra_ref.shape
    owners, _, tiles, _ = out_ref.shape
    fill_tilehot(tile_ref, hot_ref, owners * tiles)
    for k in range(blocks):
        for part in range(width // 128):
            cols = slice(part * 128, (part + 1) * 128)
            slot = k * (width // 128) + part
            for g in range(groups):
                rows_ref[slot, pl.ds(g, headings, stride=groups), :] = (
                    spectra_ref[g, k, :, cols].astype(F32)
                )
            packed_ref[:, slot * 128 : (slot + 1) * 128] = rows_ref[slot].astype(BF)
    gather_slots(hot_ref, rank_ref, packed_ref, out_ref, True)


def gather_rows(tile_ids, rank, spectra, owners, capacity):
    blocks, width = tile_ids.shape
    groups, _, headings, _ = spectra.shape
    lanes = groups * headings
    return pl.pallas_call(
        row_kernel,
        out_shape=jax.ShapeDtypeStruct((owners, capacity, TILE_DEV, lanes), BF),
        in_specs=[pl.BlockSpec(memory_space=pltpu.VMEM)] * 3,
        out_specs=pl.BlockSpec(memory_space=pltpu.VMEM),
        scratch_shapes=[
            pltpu.VMEM((owners * TILE_DEV, blocks * width), BF),
            pltpu.VMEM((blocks * width // 128, lanes, 128), F32),
            pltpu.VMEM((lanes, blocks * width), BF),
        ],
        cost_estimate=pl.CostEstimate(
            flops=2 * owners * capacity * TILE_DEV * blocks * width * lanes,
            bytes_accessed=2 << 20, transcendentals=0,
        ),
        name="row_slots",
    )(tile_ids, rank, spectra)


def node_kernel(rows_ref, weight_ref, out_ref, rows32_ref, weight32_ref):
    count, lanes = rows_ref.shape
    rows32_ref[...] = rows_ref[...].astype(F32)
    weight32_ref[...] = weight_ref[...].astype(F32)
    for tile in range(TILE_DEV):
        own = pl.ds(tile, count // TILE_DEV, stride=TILE_DEV)
        part = lax.dot_general(
            rows32_ref[own, :].astype(BF), weight32_ref[own, :].astype(BF),
            (((0,), (0,)), ((), ())), preferred_element_type=F32,
        )
        out_ref[:, tile * 128 : (tile + 1) * 128] = part.astype(BF)


def node_spectra(rows, weights):
    count, lanes = rows.shape
    return pl.pallas_call(
        node_kernel,
        out_shape=jax.ShapeDtypeStruct((lanes, TILE_DEV * 128), BF),
        in_specs=[pl.BlockSpec(memory_space=pltpu.VMEM)] * 2,
        out_specs=pl.BlockSpec(memory_space=pltpu.VMEM),
        scratch_shapes=[pltpu.VMEM((count, lanes), F32), pltpu.VMEM((count, 128), F32)],
        cost_estimate=pl.CostEstimate(
            flops=2 * count * lanes * 128, bytes_accessed=2 << 20, transcendentals=0
        ),
        name="node_spectra",
    )(rows, weights)


def history_kernel(basis_ref, *refs):
    out_ref = refs[-1]
    spectra = jnp.concatenate([r[...] for r in refs[:-1]], axis=0)
    out_ref[0] = jnp.dot(basis_ref[...], spectra, preferred_element_type=F32).astype(BF)


def histories(basis, chunks, headings):
    steps = basis.shape[0]
    lanes, nodes = chunks[0].shape
    group = lanes // headings
    return pl.pallas_call(
        history_kernel,
        grid=(headings,),
        out_shape=jax.ShapeDtypeStruct((headings, steps, nodes), BF),
        in_specs=[pl.BlockSpec(basis.shape, lambda h: (0, 0))]
        + [pl.BlockSpec((group, nodes), lambda h: (h, 0))] * len(chunks),
        out_specs=pl.BlockSpec((1, steps, nodes), lambda h: (h, 0, 0)),
        cost_estimate=pl.CostEstimate(
            flops=2 * steps * len(chunks) * lanes * nodes,
            bytes_accessed=6 << 20, transcendentals=0,
        ),
        name="histories",
    )(basis, *chunks)


def window_basis(sources, window, window_len, groups, fl_count):
    source = jnp.repeat(sources, groups)
    group = jnp.tile(jnp.arange(groups, dtype=jnp.int32), sources.shape[0])
    freq_bin = 1 + BIN_STEP * (fl_count * group + source % fl_count)
    step_ids = window * window_len + jnp.arange(window_len, dtype=jnp.int32)
    turn_count = freq_bin[None, :] * step_ids[:, None] % TSTEPS
    turn_angle = turn_count.astype(F32) * (2.0 * math.pi / TSTEPS)
    is_re = (source < fl_count)[None, :]
    return jnp.where(is_re, jnp.cos(turn_angle), -jnp.sin(turn_angle)).astype(BF)


def shards(pressure, spectrum_amp, phase_code, panel_tile, patch_weight):
    owners = lax.axis_size("freq")
    windows = lax.axis_size("node")
    group = lax.axis_index("freq")
    window = lax.axis_index("node")
    _, fl_count, headings, panels = pressure.shape
    width = panels // owners
    capacity = 12
    scaled = scale_spectra(pressure, spectrum_amp, phase_code, group, owners)
    spectra = lax.all_to_all(
        scaled.reshape(owners * windows, headings, width), ("freq", "node"), 0, 0, tiled=True
    ).reshape(owners, windows, headings, width)

    tile_ids = panel_tile.reshape(windows, width)
    weights = patch_weight.reshape(windows * width, 128)
    sent_weight, rank = gather_weights(tile_ids, weights, owners, capacity)
    got_weight = lax.all_to_all(sent_weight, "freq", 0, 0, tiled=True)

    sent_rows = gather_rows(tile_ids, rank, spectra, owners, capacity)
    got_rows = lax.all_to_all(sent_rows, "freq", 0, 0, tiled=True)
    own = node_spectra(got_rows.reshape(-1, owners * headings), got_weight.reshape(-1, 128))

    ahead = [(k, (k + 1) % windows) for k in range(windows)]
    back = [(k, (k - 1) % windows) for k in range(windows)]
    chunks, offsets = [own], [0]
    right = left = own
    for step in range(1, windows // 2 + 1):
        right_next = lax.ppermute(right, "node", ahead)
        chunks.append(right_next)
        offsets.append(-step)
        if step < windows - windows // 2:
            left = lax.ppermute(left, "node", back)
            chunks.append(left)
            offsets.append(step)
        right = right_next
    sources = (window + jnp.asarray(offsets, jnp.int32)) % windows
    basis = window_basis(sources, window, TSTEPS // windows, owners, fl_count)
    return histories(basis, chunks, headings)


def solution(mesh):
    placed = (
        P(None, "freq", None, "node"),
        P(),
        P(),
        P("freq", None, None, None),
        P("freq", None, None, None),
    )
    return jax.shard_map(
        shards, mesh=mesh, in_specs=placed, out_specs=P(None, "node", "freq"), check_vma=False
    )
```

```python
import math

import jax
import jax.numpy as jnp
from jax import lax
from jax.experimental import pallas as pl
from jax.experimental.pallas import tpu as pltpu
from jax.sharding import PartitionSpec as P

F = 128
TSTEPS = 4096
BIN_STEP = 15
PHASE_LEVELS = 4096
TILE_DEV = 8
BF = jnp.bfloat16
F32 = jnp.float32
VMEM_LIMIT = 20 << 20


def scale_kernel(group_ref, pressure_ref, amp_ref, code_ref, out_ref):
    owners, width = out_ref.shape[0], out_ref.shape[3]
    fl_count = pressure_ref.shape[1]
    lane = lax.broadcasted_iota(jnp.int32, amp_ref.shape, 1)
    angle = code_ref[...].astype(F32) * (2.0 * math.pi / PHASE_LEVELS)
    cosine, sine = jnp.cos(angle), jnp.sin(angle)
    amp = amp_ref[...]
    for fl in range(fl_count):
        chosen = lane == group_ref[0] * fl_count + fl

        def pick(table):
            return jnp.sum(jnp.where(chosen, table, 0.0), axis=1, keepdims=True)

        a, c, s = pick(amp), pick(cosine), pick(sine)

        for g in range(owners):
            cols = pl.ds(g * width, width)
            re = pressure_ref[0, fl, :, cols].astype(F32)
            im = pressure_ref[1, fl, :, cols].astype(F32)
            out_ref[g, fl] = (a * (re * c - im * s)).astype(BF)
            out_ref[g, fl_count + fl] = (a * (re * s + im * c)).astype(BF)


def scale_spectra(pressure, spectrum_amp, phase_code, group, owners):
    parts, fl_count, headings, panels = pressure.shape
    width = panels // owners
    return pl.pallas_call(
        scale_kernel,
        out_shape=jax.ShapeDtypeStruct((owners, parts * fl_count, headings, width), BF),
        in_specs=[
            pl.BlockSpec(memory_space=pltpu.SMEM),
            pl.BlockSpec(memory_space=pltpu.VMEM),
            pl.BlockSpec(memory_space=pltpu.VMEM),
            pl.BlockSpec(memory_space=pltpu.VMEM),
        ],
        out_specs=pl.BlockSpec(memory_space=pltpu.VMEM),
        cost_estimate=pl.CostEstimate(flops=2_000_000, bytes_accessed=1 << 20, transcendentals=0),
        name="scale",
    )(group.reshape(1), pressure, spectrum_amp, phase_code)


def fill_tilehot(tile_ref, hot_ref, tile_count):
    blocks, width = tile_ref.shape
    tile_iota = lax.broadcasted_iota(jnp.int32, (tile_count, width), 0)
    for k in range(blocks):
        hot = tile_iota == tile_ref[k : k + 1, :]
        hot_ref[:, k * width : (k + 1) * width] = jnp.where(hot, 1.0, 0.0).astype(BF)


def gather_slots(hot_ref, rank_ref, source_ref, out_ref):
    blocks, width = rank_ref.shape
    owners, capacity, tiles, lanes = out_ref.shape

    def one(s, carry):
        total = jnp.zeros((owners * tiles, lanes), F32)
        for k in range(blocks):
            cols = slice(k * width, (k + 1) * width)
            live = jnp.where(rank_ref[k : k + 1, :] == s.astype(F32), 1.0, 0.0).astype(BF)
            total += jnp.dot(
                hot_ref[:, cols] * live, source_ref[cols, :], preferred_element_type=F32
            )
        out_ref[:, pl.ds(s, 1)] = total.astype(BF).reshape(owners, 1, tiles, lanes)
        return carry

    lax.fori_loop(0, capacity, one, 0)


def weight_kernel(tile_ref, weight_ref, out_ref, rank_ref, hot_ref):
    owners, _, tiles, _ = out_ref.shape
    blocks, width = tile_ref.shape
    fill_tilehot(tile_ref, hot_ref, owners * tiles)
    before = (
        lax.broadcasted_iota(jnp.int32, (width, width), 0)
        < lax.broadcasted_iota(jnp.int32, (width, width), 1)
    )
    before = jnp.where(before, 1.0, 0.0).astype(BF)
    seen = jnp.zeros((owners * tiles, 1), F32)
    for k in range(blocks):
        hot = hot_ref[:, k * width : (k + 1) * width]
        hot32 = hot.astype(F32)
        earlier = jnp.dot(hot, before, preferred_element_type=F32) + seen
        rank_ref[k : k + 1, :] = jnp.sum(hot32 * earlier, axis=0, keepdims=True)
        seen = seen + jnp.sum(hot32, axis=1, keepdims=True)
    gather_slots(hot_ref, rank_ref, weight_ref, out_ref)


def gather_weights(tile_ids, weights, owners, capacity):
    blocks, width = tile_ids.shape
    lanes = weights.shape[1]
    return pl.pallas_call(
        weight_kernel,
        out_shape=(
            jax.ShapeDtypeStruct((owners, capacity, TILE_DEV, lanes), BF),
            jax.ShapeDtypeStruct((blocks, width), F32),
        ),
        in_specs=[pl.BlockSpec(memory_space=pltpu.VMEM)] * 2,
        out_specs=(pl.BlockSpec(memory_space=pltpu.VMEM),) * 2,
        scratch_shapes=[pltpu.VMEM((owners * TILE_DEV, blocks * width), BF)],
        compiler_params=pltpu.CompilerParams(vmem_limit_bytes=VMEM_LIMIT),
        cost_estimate=pl.CostEstimate(
            flops=2 * owners * capacity * TILE_DEV * blocks * width * lanes,
            bytes_accessed=2 << 20, transcendentals=0,
        ),
        name="weight_slots",
    )(tile_ids, weights)


def row_kernel(tile_ref, rank_ref, weight_ref, spectra_ref, out_ref, hot_ref, rows_ref, packed_ref):
    groups, blocks, headings, width = spectra_ref.shape
    owners, capacity, tiles, _ = out_ref.shape
    lanes = groups * headings
    parts = width // 128
    out_ref[:, :, :, lanes:] = weight_ref[...]
    fill_tilehot(tile_ref, hot_ref, owners * tiles)
    for k in range(blocks):
        for part in range(parts):
            slot = k * parts + part
            for g in range(groups):
                rows_ref[slot, pl.ds(g, headings, stride=groups), :] = (
                    spectra_ref[g, k, :, part * 128 : (part + 1) * 128].astype(F32)
                )
            packed_ref[:, slot * 128 : (slot + 1) * 128] = rows_ref[slot].astype(BF)

    def pair(step, carry):
        total = jnp.zeros((owners * tiles, 2 * lanes), F32)
        for k in range(blocks):
            cols = slice(k * width, (k + 1) * width)
            rank, rows = rank_ref[k : k + 1, :], packed_ref[:, cols]
            live = [
                jnp.where(rank == (2 * step + i).astype(F32), 1.0, 0.0).astype(BF)
                for i in range(2)
            ]
            total += lax.dot_general(
                hot_ref[:, cols], jnp.concatenate([rows * live[0], rows * live[1]], axis=0),
                (((1,), (1,)), ((), ())), preferred_element_type=F32,
            )
        for i in range(2):
            out_ref[:, pl.ds(2 * step + i, 1), :, :lanes] = (
                total[:, i * lanes : (i + 1) * lanes].astype(BF).reshape(owners, 1, tiles, lanes)
            )
        return carry

    lax.fori_loop(0, capacity // 2, pair, 0)


def gather_rows(tile_ids, rank, weights, spectra):
    blocks, width = tile_ids.shape
    groups, _, headings, _ = spectra.shape
    owners, capacity, tiles, nodes = weights.shape
    lanes = groups * headings
    return pl.pallas_call(
        row_kernel,
        out_shape=jax.ShapeDtypeStruct((owners, capacity, tiles, lanes + nodes), BF),
        in_specs=[pl.BlockSpec(memory_space=pltpu.VMEM)] * 4,
        out_specs=pl.BlockSpec(memory_space=pltpu.VMEM),
        scratch_shapes=[
            pltpu.VMEM((owners * tiles, blocks * width), BF),
            pltpu.VMEM((blocks * width // 128, lanes, 128), F32),
            pltpu.VMEM((lanes, blocks * width), BF),
        ],
        compiler_params=pltpu.CompilerParams(vmem_limit_bytes=VMEM_LIMIT),
        cost_estimate=pl.CostEstimate(
            flops=2 * owners * capacity * tiles * blocks * width * lanes,
            bytes_accessed=3 << 20, transcendentals=0,
        ),
        name="row_slots",
    )(tile_ids, rank, weights, spectra)


def node_kernel(slots_ref, out_ref, wide_ref):
    count, width = slots_ref.shape
    lanes = out_ref.shape[0]
    nodes = width - lanes
    for half in range(2):
        wide_ref[half] = slots_ref[:, half * lanes : (half + 1) * lanes].astype(F32)
    for tile in range(TILE_DEV):
        own = pl.ds(tile, count // TILE_DEV, stride=TILE_DEV)
        part = lax.dot_general(
            wide_ref[0, own, :].astype(BF), wide_ref[1, own, :].astype(BF),
            (((0,), (0,)), ((), ())), preferred_element_type=F32,
        )
        out_ref[:, tile * nodes : (tile + 1) * nodes] = part.astype(BF)


def node_spectra(slots):
    count, width = slots.shape
    lanes = width // 2
    return pl.pallas_call(
        node_kernel,
        out_shape=jax.ShapeDtypeStruct((lanes, TILE_DEV * lanes), BF),
        in_specs=[pl.BlockSpec(memory_space=pltpu.VMEM)],
        out_specs=pl.BlockSpec(memory_space=pltpu.VMEM),
        scratch_shapes=[pltpu.VMEM((2, count, lanes), F32)],
        compiler_params=pltpu.CompilerParams(vmem_limit_bytes=VMEM_LIMIT),
        cost_estimate=pl.CostEstimate(
            flops=2 * count * lanes * lanes, bytes_accessed=2 << 20, transcendentals=0
        ),
        name="node_spectra",
    )(slots)


def history_kernel(basis_ref, *refs):
    out_ref = refs[-1]
    heading = pl.program_id(0)
    group = basis_ref.shape[1] // (len(refs) - 2)
    own = pl.ds(pl.multiple_of(heading * group, group), group)
    chunks = [r[own, :] for r in refs[:-3]]
    low, high = refs[-3], refs[-2]
    half = low.shape[0] // group
    inner = pl.ds(pl.multiple_of(lax.rem(heading, half) * group, group), group)
    chunks.append(jnp.where(heading < half, low[inner, :], high[inner, :]))
    spectra = jnp.concatenate(chunks, axis=0)
    out_ref[0] = jnp.dot(basis_ref[...], spectra, preferred_element_type=F32).astype(BF)


def histories(basis, chunks, headings):
    steps = basis.shape[0]
    lanes, nodes = chunks[0].shape
    cut = 2
    return pl.pallas_call(
        history_kernel,
        grid=(headings, cut),
        out_shape=jax.ShapeDtypeStruct((headings, steps, nodes), BF),
        in_specs=[pl.BlockSpec((steps // cut, basis.shape[1]), lambda h, i: (i, 0))]
        + [pl.BlockSpec(memory_space=pltpu.VMEM)] * len(chunks),
        out_specs=pl.BlockSpec((1, steps // cut, nodes), lambda h, i: (h, i, 0)),
        compiler_params=pltpu.CompilerParams(vmem_limit_bytes=VMEM_LIMIT),
        cost_estimate=pl.CostEstimate(
            flops=2 * steps * basis.shape[1] * headings * nodes,
            bytes_accessed=6 << 20, transcendentals=0,
        ),
        name="histories",
    )(basis, *chunks)


def window_basis(sources, window, window_len, groups, fl_count):
    source = jnp.repeat(sources, groups)
    group = jnp.tile(jnp.arange(groups, dtype=jnp.int32), sources.shape[0])
    freq_bin = 1 + BIN_STEP * (fl_count * group + source % fl_count)
    step_ids = window * window_len + jnp.arange(window_len, dtype=jnp.int32)
    turn_count = freq_bin[None, :] * step_ids[:, None] % TSTEPS
    turn_angle = turn_count.astype(F32) * (2.0 * math.pi / TSTEPS)
    is_re = (source < fl_count)[None, :]
    return jnp.where(is_re, jnp.cos(turn_angle), -jnp.sin(turn_angle)).astype(BF)


def shards(pressure, spectrum_amp, phase_code, panel_tile, patch_weight):
    owners = lax.axis_size("freq")
    windows = lax.axis_size("node")
    group = lax.axis_index("freq")
    window = lax.axis_index("node")
    _, fl_count, headings, panels = pressure.shape
    width = panels // owners
    capacity = 12
    scaled = scale_spectra(pressure, spectrum_amp, phase_code, group, owners)
    spectra = lax.all_to_all(
        scaled.reshape(owners * windows, headings, width), ("freq", "node"), 0, 0, tiled=True
    ).reshape(owners, windows, headings, width)

    tile_ids = panel_tile.reshape(windows, width)
    weights = patch_weight.reshape(windows * width, 128)
    slot_weight, rank = gather_weights(tile_ids, weights, owners, capacity)
    sent = gather_rows(tile_ids, rank, slot_weight, spectra)
    got = lax.all_to_all(sent, "freq", 0, 0, tiled=True)
    own = node_spectra(got.reshape(-1, got.shape[-1]))

    def shift(chunk, distance):
        pairs = [(k, (k + distance) % windows) for k in range(windows)]
        return lax.ppermute(chunk, "node", pairs)

    half = own.shape[0] // 2
    plus2, minus2 = shift(own, 2), shift(own, -2)
    plus1, minus1 = shift(own, 1), shift(own, -1)
    plus3, minus3 = shift(plus2, 1), shift(minus2, -1)
    low4, high4 = shift(plus3[:half], 1), shift(minus3[half:], -1)
    chunks = [own, plus1, minus1, plus2, minus2, plus3, minus3, low4, high4]
    offsets = jnp.asarray([0, -1, 1, -2, 2, -3, 3, 4], jnp.int32)
    sources = (window + offsets) % windows
    basis = window_basis(sources, window, TSTEPS // windows, owners, fl_count)
    return histories(basis, chunks, headings)


def solution(mesh):
    placed = (
        P(None, "freq", None, "node"),
        P(),
        P(),
        P("freq", None, None, None),
        P("freq", None, None, None),
    )
    return jax.shard_map(
        shards, mesh=mesh, in_specs=placed, out_specs=P(None, "node", "freq"), check_vma=False
    )
```

```python
import math

import jax
import jax.numpy as jnp
from jax import lax
from jax.experimental import pallas as pl
from jax.experimental.pallas import tpu as pltpu
from jax.sharding import PartitionSpec as P

F = 128
TSTEPS = 4096
BIN_STEP = 15
PHASE_LEVELS = 4096
TILE_DEV = 8
BF = jnp.bfloat16
F32 = jnp.float32
VMEM_LIMIT = 20 << 20


def scale_kernel(group_ref, pressure_ref, amp_ref, code_ref, out_ref):
    owners, width = out_ref.shape[0], out_ref.shape[3]
    fl_count = pressure_ref.shape[1]
    lane = lax.broadcasted_iota(jnp.int32, amp_ref.shape, 1)
    angle = code_ref[...].astype(F32) * (2.0 * math.pi / PHASE_LEVELS)
    cosine, sine = jnp.cos(angle), jnp.sin(angle)
    amp = amp_ref[...]
    for fl in range(fl_count):
        chosen = lane == group_ref[0] * fl_count + fl

        def pick(table):
            return jnp.sum(jnp.where(chosen, table, 0.0), axis=1, keepdims=True)

        a, c, s = pick(amp), pick(cosine), pick(sine)

        for g in range(owners):
            cols = pl.ds(g * width, width)
            re = pressure_ref[0, fl, :, cols].astype(F32)
            im = pressure_ref[1, fl, :, cols].astype(F32)
            out_ref[g, fl] = (a * (re * c - im * s)).astype(BF)
            out_ref[g, fl_count + fl] = (a * (re * s + im * c)).astype(BF)


def scale_spectra(pressure, spectrum_amp, phase_code, group, owners):
    parts, fl_count, headings, panels = pressure.shape
    width = panels // owners
    return pl.pallas_call(
        scale_kernel,
        out_shape=jax.ShapeDtypeStruct((owners, parts * fl_count, headings, width), BF),
        in_specs=[
            pl.BlockSpec(memory_space=pltpu.SMEM),
            pl.BlockSpec(memory_space=pltpu.VMEM),
            pl.BlockSpec(memory_space=pltpu.VMEM),
            pl.BlockSpec(memory_space=pltpu.VMEM),
        ],
        out_specs=pl.BlockSpec(memory_space=pltpu.VMEM),
        cost_estimate=pl.CostEstimate(flops=2_000_000, bytes_accessed=1 << 20, transcendentals=0),
        name="scale",
    )(group.reshape(1), pressure, spectrum_amp, phase_code)


def fill_tilehot(tile_ref, hot_ref, tile_count):
    blocks, width = tile_ref.shape
    tile_iota = lax.broadcasted_iota(jnp.int32, (tile_count, width), 0)
    for k in range(blocks):
        hot = tile_iota == tile_ref[k : k + 1, :]
        hot_ref[:, k * width : (k + 1) * width] = jnp.where(hot, 1.0, 0.0).astype(BF)


def gather_slots(hot_ref, rank_ref, source_ref, out_ref):
    blocks, width = rank_ref.shape
    owners, capacity, tiles, lanes = out_ref.shape

    def one(s, carry):
        total = jnp.zeros((owners * tiles, lanes), F32)
        for k in range(blocks):
            cols = slice(k * width, (k + 1) * width)
            live = jnp.where(rank_ref[k : k + 1, :] == s.astype(F32), 1.0, 0.0).astype(BF)
            total += jnp.dot(
                hot_ref[:, cols] * live, source_ref[cols, :], preferred_element_type=F32
            )
        out_ref[:, pl.ds(s, 1)] = total.astype(BF).reshape(owners, 1, tiles, lanes)
        return carry

    lax.fori_loop(0, capacity, one, 0)


def weight_kernel(tile_ref, weight_ref, out_ref, rank_ref, hot_ref):
    owners, _, tiles, _ = out_ref.shape
    blocks, width = tile_ref.shape
    fill_tilehot(tile_ref, hot_ref, owners * tiles)
    before = (
        lax.broadcasted_iota(jnp.int32, (width, width), 0)
        < lax.broadcasted_iota(jnp.int32, (width, width), 1)
    )
    before = jnp.where(before, 1.0, 0.0).astype(BF)
    seen = jnp.zeros((owners * tiles, 1), F32)
    for k in range(blocks):
        hot = hot_ref[:, k * width : (k + 1) * width]
        hot32 = hot.astype(F32)
        earlier = jnp.dot(hot, before, preferred_element_type=F32) + seen
        rank_ref[k : k + 1, :] = jnp.sum(hot32 * earlier, axis=0, keepdims=True)
        seen = seen + jnp.sum(hot32, axis=1, keepdims=True)
    gather_slots(hot_ref, rank_ref, weight_ref, out_ref)


def gather_weights(tile_ids, weights, owners, capacity):
    blocks, width = tile_ids.shape
    lanes = weights.shape[1]
    return pl.pallas_call(
        weight_kernel,
        out_shape=(
            jax.ShapeDtypeStruct((owners, capacity, TILE_DEV, lanes), BF),
            jax.ShapeDtypeStruct((blocks, width), F32),
            jax.ShapeDtypeStruct((owners * TILE_DEV, blocks * width), BF),
        ),
        in_specs=[pl.BlockSpec(memory_space=pltpu.VMEM)] * 2,
        out_specs=(pl.BlockSpec(memory_space=pltpu.VMEM),) * 3,
        compiler_params=pltpu.CompilerParams(vmem_limit_bytes=VMEM_LIMIT),
        cost_estimate=pl.CostEstimate(
            flops=2 * owners * capacity * TILE_DEV * blocks * width * lanes,
            bytes_accessed=2 << 20, transcendentals=0,
        ),
        name="weight_slots",
    )(tile_ids, weights)


def row_kernel(hot_ref, rank_ref, weight_ref, spectra_ref, out_ref, rows_ref, packed_ref, masked_ref):
    groups, blocks, headings, width = spectra_ref.shape
    owners, capacity, tiles, _ = out_ref.shape
    lanes = groups * headings
    parts = width // 128
    out_ref[:, :, :, lanes:] = weight_ref[...]
    for k in range(blocks):
        for part in range(parts):
            slot = k * parts + part
            for g in range(groups):
                rows_ref[slot, pl.ds(g, headings, stride=groups), :] = (
                    spectra_ref[g, k, :, part * 128 : (part + 1) * 128].astype(F32)
                )
            packed_ref[:, slot * 128 : (slot + 1) * 128] = rows_ref[slot].astype(BF)

    def pair(step, carry):
        for k in range(blocks):
            cols = slice(k * width, (k + 1) * width)
            rank, rows = rank_ref[k : k + 1, :], packed_ref[:, cols]
            for i in range(2):
                live = jnp.where(rank == (2 * step + i).astype(F32), 1.0, 0.0).astype(BF)
                masked_ref[i * lanes : (i + 1) * lanes, cols] = rows * live
        total = lax.dot_general(
            hot_ref[...], masked_ref[...], (((1,), (1,)), ((), ())), preferred_element_type=F32
        )
        for i in range(2):
            out_ref[:, pl.ds(2 * step + i, 1), :, :lanes] = (
                total[:, i * lanes : (i + 1) * lanes].astype(BF).reshape(owners, 1, tiles, lanes)
            )
        return carry

    lax.fori_loop(0, capacity // 2, pair, 0)


def gather_rows(hot, rank, weights, spectra):
    blocks, width = rank.shape
    groups, _, headings, _ = spectra.shape
    owners, capacity, tiles, nodes = weights.shape
    lanes = groups * headings
    return pl.pallas_call(
        row_kernel,
        out_shape=jax.ShapeDtypeStruct((owners, capacity, tiles, lanes + nodes), BF),
        in_specs=[pl.BlockSpec(memory_space=pltpu.VMEM)] * 4,
        out_specs=pl.BlockSpec(memory_space=pltpu.VMEM),
        scratch_shapes=[
            pltpu.VMEM((blocks * width // 128, lanes, 128), F32),
            pltpu.VMEM((lanes, blocks * width), BF),
            pltpu.VMEM((2 * lanes, blocks * width), BF),
        ],
        compiler_params=pltpu.CompilerParams(vmem_limit_bytes=VMEM_LIMIT),
        cost_estimate=pl.CostEstimate(
            flops=2 * owners * capacity * tiles * blocks * width * lanes,
            bytes_accessed=3 << 20, transcendentals=0,
        ),
        name="row_slots",
    )(hot, rank, weights, spectra)


def node_kernel(slots_ref, out_ref, wide_ref):
    count, width = slots_ref.shape
    lanes = out_ref.shape[0]
    nodes = width - lanes
    for half in range(2):
        wide_ref[half] = slots_ref[:, half * lanes : (half + 1) * lanes].astype(F32)
    for tile in range(TILE_DEV):
        own = pl.ds(tile, count // TILE_DEV, stride=TILE_DEV)
        part = lax.dot_general(
            wide_ref[0, own, :].astype(BF), wide_ref[1, own, :].astype(BF),
            (((0,), (0,)), ((), ())), preferred_element_type=F32,
        )
        out_ref[:, tile * nodes : (tile + 1) * nodes] = part.astype(BF)


def node_spectra(slots):
    count, width = slots.shape
    lanes = width // 2
    return pl.pallas_call(
        node_kernel,
        out_shape=jax.ShapeDtypeStruct((lanes, TILE_DEV * lanes), BF),
        in_specs=[pl.BlockSpec(memory_space=pltpu.VMEM)],
        out_specs=pl.BlockSpec(memory_space=pltpu.VMEM),
        scratch_shapes=[pltpu.VMEM((2, count, lanes), F32)],
        compiler_params=pltpu.CompilerParams(vmem_limit_bytes=VMEM_LIMIT),
        cost_estimate=pl.CostEstimate(
            flops=2 * count * lanes * lanes, bytes_accessed=2 << 20, transcendentals=0
        ),
        name="node_spectra",
    )(slots)


def history_kernel(basis_ref, *refs):
    out_ref = refs[-1]
    heading = pl.program_id(0)
    group = basis_ref.shape[1] // (len(refs) - 2)
    own = pl.ds(pl.multiple_of(heading * group, group), group)
    nodes = out_ref.shape[2]
    cols = pl.ds(pl.multiple_of(pl.program_id(1) * nodes, nodes), nodes)
    chunks = [r[own, cols] for r in refs[:-3]]
    low, high = refs[-3], refs[-2]
    half = low.shape[0] // group
    inner = pl.ds(pl.multiple_of(lax.rem(heading, half) * group, group), group)
    chunks.append(jnp.where(heading < half, low[inner, cols], high[inner, cols]))
    spectra = jnp.concatenate(chunks, axis=0)
    out_ref[0] = jnp.dot(basis_ref[...], spectra, preferred_element_type=F32).astype(BF)


def histories(basis, chunks, headings):
    steps = basis.shape[0]
    lanes, nodes = chunks[0].shape
    cut = 2
    return pl.pallas_call(
        history_kernel,
        grid=(headings, cut),
        out_shape=jax.ShapeDtypeStruct((headings, steps, nodes), BF),
        in_specs=[pl.BlockSpec(memory_space=pltpu.VMEM)] * (1 + len(chunks)),
        out_specs=pl.BlockSpec((1, steps, nodes // cut), lambda h, i: (h, 0, i)),
        compiler_params=pltpu.CompilerParams(vmem_limit_bytes=VMEM_LIMIT),
        cost_estimate=pl.CostEstimate(
            flops=2 * steps * basis.shape[1] * headings * nodes,
            bytes_accessed=6 << 20, transcendentals=0,
        ),
        name="histories",
    )(basis, *chunks)


def window_basis(sources, window, window_len, groups, fl_count):
    source = jnp.repeat(sources, groups)
    group = jnp.tile(jnp.arange(groups, dtype=jnp.int32), sources.shape[0])
    freq_bin = 1 + BIN_STEP * (fl_count * group + source % fl_count)
    step_ids = window * window_len + jnp.arange(window_len, dtype=jnp.int32)
    turn_count = freq_bin[None, :] * step_ids[:, None] % TSTEPS
    turn_angle = turn_count.astype(F32) * (2.0 * math.pi / TSTEPS)
    is_re = (source < fl_count)[None, :]
    return jnp.where(is_re, jnp.cos(turn_angle), -jnp.sin(turn_angle)).astype(BF)


def shards(pressure, spectrum_amp, phase_code, panel_tile, patch_weight):
    owners = lax.axis_size("freq")
    windows = lax.axis_size("node")
    group = lax.axis_index("freq")
    window = lax.axis_index("node")
    _, fl_count, headings, panels = pressure.shape
    width = panels // owners
    capacity = 12
    scaled = scale_spectra(pressure, spectrum_amp, phase_code, group, owners)
    spectra = lax.all_to_all(
        scaled.reshape(owners * windows, headings, width), ("freq", "node"), 0, 0, tiled=True
    ).reshape(owners, windows, headings, width)

    tile_ids = panel_tile.reshape(windows, width)
    weights = patch_weight.reshape(windows * width, 128)
    slot_weight, rank, hot = gather_weights(tile_ids, weights, owners, capacity)
    sent = gather_rows(hot, rank, slot_weight, spectra)
    got = lax.all_to_all(sent, "freq", 0, 0, tiled=True)
    own = node_spectra(got.reshape(-1, got.shape[-1]))

    def shift(chunk, distance):
        pairs = [(k, (k + distance) % windows) for k in range(windows)]
        return lax.ppermute(chunk, "node", pairs)

    half = own.shape[0] // 2
    plus1, minus1 = shift(own, 1), shift(own, -1)
    plus2, minus2 = shift(own, 2), shift(own, -2)
    plus3, minus3 = shift(plus1, 2), shift(minus1, -2)
    low4, high4 = shift(plus2[:half], 2), shift(minus2[half:], -2)
    chunks = [own, plus1, minus1, plus2, minus2, plus3, minus3, low4, high4]
    offsets = jnp.asarray([0, -1, 1, -2, 2, -3, 3, 4], jnp.int32)
    sources = (window + offsets) % windows
    basis = window_basis(sources, window, TSTEPS // windows, owners, fl_count)
    return histories(basis, chunks, headings)


def solution(mesh):
    placed = (
        P(None, "freq", None, "node"),
        P(),
        P(),
        P("freq", None, None, None),
        P("freq", None, None, None),
    )
    return jax.shard_map(
        shards, mesh=mesh, in_specs=placed, out_specs=P(None, "node", "freq"), check_vma=False
    )
```

```python
import math

import jax
import jax.numpy as jnp
from jax import lax
from jax.experimental import pallas as pl
from jax.experimental.pallas import tpu as pltpu
from jax.sharding import PartitionSpec as P

F = 128
TSTEPS = 4096
BIN_STEP = 15
PHASE_LEVELS = 4096
TILE_DEV = 8
BF = jnp.bfloat16
F32 = jnp.float32
VMEM_LIMIT = 20 << 20


def scale_kernel(group_ref, pressure_ref, amp_ref, code_ref, out_ref):
    owners, width = out_ref.shape[0], out_ref.shape[3]
    fl_count = pressure_ref.shape[1]
    lane = lax.broadcasted_iota(jnp.int32, amp_ref.shape, 1)
    angle = code_ref[...].astype(F32) * (2.0 * math.pi / PHASE_LEVELS)
    cosine, sine = jnp.cos(angle), jnp.sin(angle)
    amp = amp_ref[...]
    for fl in range(fl_count):
        chosen = lane == group_ref[0] * fl_count + fl

        def pick(table):
            return jnp.sum(jnp.where(chosen, table, 0.0), axis=1, keepdims=True)

        a, c, s = pick(amp), pick(cosine), pick(sine)

        for g in range(owners):
            cols = pl.ds(g * width, width)
            re = pressure_ref[0, fl, :, cols].astype(F32)
            im = pressure_ref[1, fl, :, cols].astype(F32)
            out_ref[g, fl] = (a * (re * c - im * s)).astype(BF)
            out_ref[g, fl_count + fl] = (a * (re * s + im * c)).astype(BF)


def scale_spectra(pressure, spectrum_amp, phase_code, group, owners):
    parts, fl_count, headings, panels = pressure.shape
    width = panels // owners
    return pl.pallas_call(
        scale_kernel,
        out_shape=jax.ShapeDtypeStruct((owners, parts * fl_count, headings, width), BF),
        in_specs=[
            pl.BlockSpec(memory_space=pltpu.SMEM),
            pl.BlockSpec(memory_space=pltpu.VMEM),
            pl.BlockSpec(memory_space=pltpu.VMEM),
            pl.BlockSpec(memory_space=pltpu.VMEM),
        ],
        out_specs=pl.BlockSpec(memory_space=pltpu.VMEM),
        cost_estimate=pl.CostEstimate(flops=2_000_000, bytes_accessed=1 << 20, transcendentals=0),
        name="scale",
    )(group.reshape(1), pressure, spectrum_amp, phase_code)


def fill_tilehot(tile_ref, hot_ref, tile_count):
    blocks, width = tile_ref.shape
    tile_iota = lax.broadcasted_iota(jnp.int32, (tile_count, width), 0)
    for k in range(blocks):
        hot = tile_iota == tile_ref[k : k + 1, :]
        hot_ref[:, k * width : (k + 1) * width] = jnp.where(hot, 1.0, 0.0).astype(BF)


def gather_slots(hot_ref, rank_ref, source_ref, out_ref):
    blocks, width = rank_ref.shape
    owners, capacity, tiles, lanes = out_ref.shape

    def one(s, carry):
        total = jnp.zeros((owners * tiles, lanes), F32)
        for k in range(blocks):
            cols = slice(k * width, (k + 1) * width)
            live = jnp.where(rank_ref[k : k + 1, :] == s.astype(F32), 1.0, 0.0).astype(BF)
            total += jnp.dot(
                hot_ref[:, cols] * live, source_ref[cols, :], preferred_element_type=F32
            )
        out_ref[:, pl.ds(s, 1)] = total.astype(BF).reshape(owners, 1, tiles, lanes)
        return carry

    lax.fori_loop(0, capacity, one, 0)


def weight_kernel(tile_ref, weight_ref, out_ref, rank_ref, hot_ref):
    owners, _, tiles, _ = out_ref.shape
    blocks, width = tile_ref.shape
    fill_tilehot(tile_ref, hot_ref, owners * tiles)
    before = (
        lax.broadcasted_iota(jnp.int32, (width, width), 0)
        < lax.broadcasted_iota(jnp.int32, (width, width), 1)
    )
    before = jnp.where(before, 1.0, 0.0).astype(BF)
    seen = jnp.zeros((owners * tiles, 1), F32)
    for k in range(blocks):
        hot = hot_ref[:, k * width : (k + 1) * width]
        hot32 = hot.astype(F32)
        earlier = jnp.dot(hot, before, preferred_element_type=F32) + seen
        rank_ref[k : k + 1, :] = jnp.sum(hot32 * earlier, axis=0, keepdims=True)
        seen = seen + jnp.sum(hot32, axis=1, keepdims=True)
    gather_slots(hot_ref, rank_ref, weight_ref, out_ref)


def gather_weights(tile_ids, weights, owners, capacity):
    blocks, width = tile_ids.shape
    lanes = weights.shape[1]
    return pl.pallas_call(
        weight_kernel,
        out_shape=(
            jax.ShapeDtypeStruct((owners, capacity, TILE_DEV, lanes), BF),
            jax.ShapeDtypeStruct((blocks, width), F32),
            jax.ShapeDtypeStruct((owners * TILE_DEV, blocks * width), BF),
        ),
        in_specs=[pl.BlockSpec(memory_space=pltpu.VMEM)] * 2,
        out_specs=(pl.BlockSpec(memory_space=pltpu.VMEM),) * 3,
        compiler_params=pltpu.CompilerParams(vmem_limit_bytes=VMEM_LIMIT),
        cost_estimate=pl.CostEstimate(
            flops=2 * owners * capacity * TILE_DEV * blocks * width * lanes,
            bytes_accessed=2 << 20, transcendentals=0,
        ),
        name="weight_slots",
    )(tile_ids, weights)


def row_kernel(hot_ref, rank_ref, weight_ref, spectra_ref, out_ref, rows_ref, packed_ref, masked_ref):
    groups, blocks, headings, width = spectra_ref.shape
    owners, capacity, tiles, _ = out_ref.shape
    lanes = groups * headings
    parts = width // 128
    out_ref[:, :, :, lanes:] = weight_ref[...]
    for k in range(blocks):
        for part in range(parts):
            slot = k * parts + part
            for g in range(groups):
                rows_ref[slot, pl.ds(g, headings, stride=groups), :] = (
                    spectra_ref[g, k, :, part * 128 : (part + 1) * 128].astype(F32)
                )
            packed_ref[:, slot * 128 : (slot + 1) * 128] = rows_ref[slot].astype(BF)

    def pair(step, carry):
        for k in range(blocks):
            cols = slice(k * width, (k + 1) * width)
            rank, rows = rank_ref[k : k + 1, :], packed_ref[:, cols]
            for i in range(2):
                live = jnp.where(rank == (2 * step + i).astype(F32), 1.0, 0.0).astype(BF)
                masked_ref[i * lanes : (i + 1) * lanes, cols] = rows * live
        total = lax.dot_general(
            hot_ref[...], masked_ref[...], (((1,), (1,)), ((), ())), preferred_element_type=F32
        )
        for i in range(2):
            out_ref[:, pl.ds(2 * step + i, 1), :, :lanes] = (
                total[:, i * lanes : (i + 1) * lanes].astype(BF).reshape(owners, 1, tiles, lanes)
            )
        return carry

    lax.fori_loop(0, capacity // 2, pair, 0)


def gather_rows(hot, rank, weights, spectra):
    blocks, width = rank.shape
    groups, _, headings, _ = spectra.shape
    owners, capacity, tiles, nodes = weights.shape
    lanes = groups * headings
    return pl.pallas_call(
        row_kernel,
        out_shape=jax.ShapeDtypeStruct((owners, capacity, tiles, lanes + nodes), BF),
        in_specs=[pl.BlockSpec(memory_space=pltpu.VMEM)] * 4,
        out_specs=pl.BlockSpec(memory_space=pltpu.VMEM),
        scratch_shapes=[
            pltpu.VMEM((blocks * width // 128, lanes, 128), F32),
            pltpu.VMEM((lanes, blocks * width), BF),
            pltpu.VMEM((2 * lanes, blocks * width), BF),
        ],
        compiler_params=pltpu.CompilerParams(vmem_limit_bytes=VMEM_LIMIT),
        cost_estimate=pl.CostEstimate(
            flops=2 * owners * capacity * tiles * blocks * width * lanes,
            bytes_accessed=3 << 20, transcendentals=0,
        ),
        name="row_slots",
    )(hot, rank, weights, spectra)


def node_kernel(slots_ref, low_ref, high_ref, wide_ref):
    count, width = slots_ref.shape
    half_lanes = low_ref.shape[0]
    lanes = 2 * half_lanes
    nodes = width - lanes
    for half in range(2):
        wide_ref[half] = slots_ref[:, half * lanes : (half + 1) * lanes].astype(F32)
    for tile in range(TILE_DEV):
        own = pl.ds(tile, count // TILE_DEV, stride=TILE_DEV)
        part = lax.dot_general(
            wide_ref[0, own, :].astype(BF), wide_ref[1, own, :].astype(BF),
            (((0,), (0,)), ((), ())), preferred_element_type=F32,
        )
        low_ref[:, tile * nodes : (tile + 1) * nodes] = part[:half_lanes].astype(BF)
        high_ref[:, tile * nodes : (tile + 1) * nodes] = part[half_lanes:].astype(BF)


def node_spectra(slots):
    count, width = slots.shape
    lanes = width // 2
    return pl.pallas_call(
        node_kernel,
        out_shape=(jax.ShapeDtypeStruct((lanes // 2, TILE_DEV * lanes), BF),) * 2,
        in_specs=[pl.BlockSpec(memory_space=pltpu.VMEM)],
        out_specs=(pl.BlockSpec(memory_space=pltpu.VMEM),) * 2,
        scratch_shapes=[pltpu.VMEM((2, count, lanes), F32)],
        compiler_params=pltpu.CompilerParams(vmem_limit_bytes=VMEM_LIMIT),
        cost_estimate=pl.CostEstimate(
            flops=2 * count * lanes * lanes, bytes_accessed=2 << 20, transcendentals=0
        ),
        name="node_spectra",
    )(slots)


def history_kernel(basis_ref, *refs):
    spectra_refs, out_ref = refs[:-1], refs[-1]
    count = len(spectra_refs) // 2
    group = basis_ref.shape[1] // count
    half = spectra_refs[0].shape[0] // group
    heading = pl.program_id(0)
    own = pl.ds(pl.multiple_of(lax.rem(heading, half) * group, group), group)
    nodes = out_ref.shape[2]
    cols = pl.ds(pl.multiple_of(pl.program_id(1) * nodes, nodes), nodes)
    for part in range(2):

        @pl.when(heading // half == part)
        def _():
            chunks = [r[own, cols] for r in spectra_refs[part * count : (part + 1) * count]]
            spectra = jnp.concatenate(chunks, axis=0)
            out_ref[0] = jnp.dot(basis_ref[...], spectra, preferred_element_type=F32).astype(BF)


def histories(basis, chunks, headings):
    steps = basis.shape[0]
    nodes = chunks[0].shape[1]
    cut = 2
    return pl.pallas_call(
        history_kernel,
        grid=(headings, cut),
        out_shape=jax.ShapeDtypeStruct((headings, steps, nodes), BF),
        in_specs=[pl.BlockSpec(memory_space=pltpu.VMEM)] * (1 + len(chunks)),
        out_specs=pl.BlockSpec((1, steps, nodes // cut), lambda h, i: (h, 0, i)),
        compiler_params=pltpu.CompilerParams(vmem_limit_bytes=VMEM_LIMIT),
        cost_estimate=pl.CostEstimate(
            flops=2 * steps * basis.shape[1] * headings * nodes,
            bytes_accessed=6 << 20, transcendentals=0,
        ),
        name="histories",
    )(basis, *chunks)


def window_basis(sources, window, window_len, groups, fl_count):
    source = jnp.repeat(sources, groups)
    group = jnp.tile(jnp.arange(groups, dtype=jnp.int32), sources.shape[0])
    freq_bin = 1 + BIN_STEP * (fl_count * group + source % fl_count)
    step_ids = window * window_len + jnp.arange(window_len, dtype=jnp.int32)
    turn_count = freq_bin[None, :] * step_ids[:, None] % TSTEPS
    turn_angle = turn_count.astype(F32) * (2.0 * math.pi / TSTEPS)
    is_re = (source < fl_count)[None, :]
    return jnp.where(is_re, jnp.cos(turn_angle), -jnp.sin(turn_angle)).astype(BF)


def shards(pressure, spectrum_amp, phase_code, panel_tile, patch_weight):
    owners = lax.axis_size("freq")
    windows = lax.axis_size("node")
    group = lax.axis_index("freq")
    window = lax.axis_index("node")
    _, fl_count, headings, panels = pressure.shape
    width = panels // owners
    capacity = 12
    scaled = scale_spectra(pressure, spectrum_amp, phase_code, group, owners)
    spectra = lax.all_to_all(
        scaled.reshape(owners * windows, headings, width), ("freq", "node"), 0, 0, tiled=True
    ).reshape(owners, windows, headings, width)

    tile_ids = panel_tile.reshape(windows, width)
    weights = patch_weight.reshape(windows * width, 128)
    slot_weight, rank, hot = gather_weights(tile_ids, weights, owners, capacity)
    sent = gather_rows(hot, rank, slot_weight, spectra)
    got = lax.all_to_all(sent, "freq", 0, 0, tiled=True)
    low, high = node_spectra(got.reshape(-1, got.shape[-1]))

    def shift(chunk, distance):
        pairs = [(k, (k + distance) % windows) for k in range(windows)]
        return lax.ppermute(chunk, "node", pairs)

    lows, highs, offsets = [low], [high], [0]
    low_up = low_down = low
    high_up = high_down = high
    for step in range(1, windows // 2):
        low_up = shift(low_up, 1)
        high_down = shift(high_down, -1)
        high_up = shift(high_up, 1)
        low_down = shift(low_down, -1)
        lows += [low_up, low_down]
        highs += [high_up, high_down]
        offsets += [-step, step]
    chunks = lows + [shift(low_up, 1)] + highs + [shift(high_down, -1)]
    offsets = jnp.asarray(offsets + [windows // 2], jnp.int32)
    sources = (window + offsets) % windows
    basis = window_basis(sources, window, TSTEPS // windows, owners, fl_count)
    return histories(basis, chunks, headings)


def solution(mesh):
    placed = (
        P(None, "freq", None, "node"),
        P(),
        P(),
        P("freq", None, None, None),
        P("freq", None, None, None),
    )
    return jax.shard_map(
        shards, mesh=mesh, in_specs=placed, out_specs=P(None, "node", "freq"), check_vma=False
    )
```

```python
import functools
import math

import jax
import jax.numpy as jnp
from jax import lax
from jax.experimental import pallas as pl
from jax.experimental.pallas import tpu as pltpu
from jax.sharding import PartitionSpec as P

F = 128
TSTEPS = 4096
BIN_STEP = 15
PHASE_LEVELS = 4096
TILE_DEV = 8
BF = jnp.bfloat16
F32 = jnp.float32
VMEM_LIMIT = 20 << 20


def scale_kernel(group_ref, pressure_ref, amp_ref, code_ref, out_ref):
    owners, width = out_ref.shape[0], out_ref.shape[3]
    fl_count = pressure_ref.shape[1]
    lane = lax.broadcasted_iota(jnp.int32, amp_ref.shape, 1)
    angle = code_ref[...].astype(F32) * (2.0 * math.pi / PHASE_LEVELS)
    cosine, sine = jnp.cos(angle), jnp.sin(angle)
    amp = amp_ref[...]
    for fl in range(fl_count):
        chosen = lane == group_ref[0] * fl_count + fl

        def pick(table):
            return jnp.sum(jnp.where(chosen, table, 0.0), axis=1, keepdims=True)

        a, c, s = pick(amp), pick(cosine), pick(sine)

        for g in range(owners):
            cols = pl.ds(g * width, width)
            re = pressure_ref[0, fl, :, cols].astype(F32)
            im = pressure_ref[1, fl, :, cols].astype(F32)
            out_ref[g, fl] = (a * (re * c - im * s)).astype(BF)
            out_ref[g, fl_count + fl] = (a * (re * s + im * c)).astype(BF)


def scale_spectra(pressure, spectrum_amp, phase_code, group, owners):
    parts, fl_count, headings, panels = pressure.shape
    width = panels // owners
    return pl.pallas_call(
        scale_kernel,
        out_shape=jax.ShapeDtypeStruct((owners, parts * fl_count, headings, width), BF),
        in_specs=[
            pl.BlockSpec(memory_space=pltpu.SMEM),
            pl.BlockSpec(memory_space=pltpu.VMEM),
            pl.BlockSpec(memory_space=pltpu.VMEM),
            pl.BlockSpec(memory_space=pltpu.VMEM),
        ],
        out_specs=pl.BlockSpec(memory_space=pltpu.VMEM),
        cost_estimate=pl.CostEstimate(flops=2_000_000, bytes_accessed=1 << 20, transcendentals=0),
        name="scale",
    )(group.reshape(1), pressure, spectrum_amp, phase_code)


def fill_tilehot(tile_ref, hot_ref, tile_count):
    blocks, width = tile_ref.shape
    tile_iota = lax.broadcasted_iota(jnp.int32, (tile_count, width), 0)
    for k in range(blocks):
        hot = tile_iota == tile_ref[k : k + 1, :]
        hot_ref[:, k * width : (k + 1) * width] = jnp.where(hot, 1.0, 0.0).astype(BF)


def gather_slots(hot_ref, rank_ref, source_ref, out_ref):
    blocks, width = rank_ref.shape
    owners, capacity, tiles, lanes = out_ref.shape

    def one(s, carry):
        total = jnp.zeros((owners * tiles, lanes), F32)
        for k in range(blocks):
            cols = slice(k * width, (k + 1) * width)
            live = jnp.where(rank_ref[k : k + 1, :] == s.astype(F32), 1.0, 0.0).astype(BF)
            total += jnp.dot(
                hot_ref[:, cols] * live, source_ref[cols, :], preferred_element_type=F32
            )
        out_ref[:, pl.ds(s, 1)] = total.astype(BF).reshape(owners, 1, tiles, lanes)
        return carry

    lax.fori_loop(0, capacity, one, 0)


def weight_kernel(tile_ref, weight_ref, out_ref, rank_ref, hot_ref):
    owners, _, tiles, _ = out_ref.shape
    blocks, width = tile_ref.shape
    fill_tilehot(tile_ref, hot_ref, owners * tiles)
    before = (
        lax.broadcasted_iota(jnp.int32, (width, width), 0)
        < lax.broadcasted_iota(jnp.int32, (width, width), 1)
    )
    before = jnp.where(before, 1.0, 0.0).astype(BF)
    seen = jnp.zeros((owners * tiles, 1), F32)
    for k in range(blocks):
        hot = hot_ref[:, k * width : (k + 1) * width]
        hot32 = hot.astype(F32)
        earlier = jnp.dot(hot, before, preferred_element_type=F32) + seen
        rank_ref[k : k + 1, :] = jnp.sum(hot32 * earlier, axis=0, keepdims=True)
        seen = seen + jnp.sum(hot32, axis=1, keepdims=True)
    gather_slots(hot_ref, rank_ref, weight_ref, out_ref)


def gather_weights(tile_ids, weights, owners, capacity):
    blocks, width = tile_ids.shape
    lanes = weights.shape[1]
    return pl.pallas_call(
        weight_kernel,
        out_shape=(
            jax.ShapeDtypeStruct((owners, capacity, TILE_DEV, lanes), BF),
            jax.ShapeDtypeStruct((blocks, width), F32),
            jax.ShapeDtypeStruct((owners * TILE_DEV, blocks * width), BF),
        ),
        in_specs=[pl.BlockSpec(memory_space=pltpu.VMEM)] * 2,
        out_specs=(pl.BlockSpec(memory_space=pltpu.VMEM),) * 3,
        compiler_params=pltpu.CompilerParams(vmem_limit_bytes=VMEM_LIMIT),
        cost_estimate=pl.CostEstimate(
            flops=2 * owners * capacity * TILE_DEV * blocks * width * lanes,
            bytes_accessed=2 << 20, transcendentals=0,
        ),
        name="weight_slots",
    )(tile_ids, weights)


def row_kernel(hot_ref, rank_ref, weight_ref, spectra_ref, out_ref, rows_ref, packed_ref, masked_ref):
    groups, blocks, headings, width = spectra_ref.shape
    owners, capacity, tiles, _ = out_ref.shape
    lanes = groups * headings
    parts = width // 128
    out_ref[:, :, :, lanes:] = weight_ref[...]
    for k in range(blocks):
        for part in range(parts):
            slot = k * parts + part
            for g in range(groups):
                rows_ref[slot, pl.ds(g, headings, stride=groups), :] = (
                    spectra_ref[g, k, :, part * 128 : (part + 1) * 128].astype(F32)
                )
            packed_ref[:, slot * 128 : (slot + 1) * 128] = rows_ref[slot].astype(BF)

    for step in range(capacity // 2):
        for k in range(blocks):
            cols = slice(k * width, (k + 1) * width)
            rank, rows = rank_ref[k : k + 1, :], packed_ref[:, cols]
            for i in range(2):
                live = jnp.where(rank == float(2 * step + i), 1.0, 0.0).astype(BF)
                masked_ref[i * lanes : (i + 1) * lanes, cols] = rows * live
        total = lax.dot_general(
            hot_ref[...], masked_ref[...], (((1,), (1,)), ((), ())), preferred_element_type=F32
        )
        for i in range(2):
            out_ref[:, 2 * step + i, :, :lanes] = (
                total[:, i * lanes : (i + 1) * lanes].astype(BF).reshape(owners, tiles, lanes)
            )


def gather_rows(hot, rank, weights, spectra):
    blocks, width = rank.shape
    groups, _, headings, _ = spectra.shape
    owners, capacity, tiles, nodes = weights.shape
    lanes = groups * headings
    return pl.pallas_call(
        row_kernel,
        out_shape=pltpu.VMEM((owners, capacity, tiles, lanes + nodes), BF),
        in_specs=[pl.BlockSpec(memory_space=pltpu.VMEM)] * 4,
        out_specs=pl.BlockSpec(memory_space=pltpu.VMEM),
        scratch_shapes=[
            pltpu.VMEM((blocks * width // 128, lanes, 128), F32),
            pltpu.VMEM((lanes, blocks * width), BF),
            pltpu.VMEM((2 * lanes, blocks * width), BF),
        ],
        compiler_params=pltpu.CompilerParams(vmem_limit_bytes=VMEM_LIMIT),
        cost_estimate=pl.CostEstimate(
            flops=2 * owners * capacity * tiles * blocks * width * lanes,
            bytes_accessed=3 << 20, transcendentals=0,
        ),
        name="row_slots",
    )(hot, rank, weights, spectra)


def node_kernel(slots_ref, low_ref, high_ref, wide_ref):
    count, width = slots_ref.shape
    half_lanes = low_ref.shape[0]
    lanes = 2 * half_lanes
    nodes = width - lanes
    for half in range(2):
        wide_ref[half] = slots_ref[:, half * lanes : (half + 1) * lanes].astype(F32)
    for tile in range(TILE_DEV):
        own = pl.ds(tile, count // TILE_DEV, stride=TILE_DEV)
        part = lax.dot_general(
            wide_ref[0, own, :].astype(BF), wide_ref[1, own, :].astype(BF),
            (((0,), (0,)), ((), ())), preferred_element_type=F32,
        )
        low_ref[:, tile * nodes : (tile + 1) * nodes] = part[:half_lanes].astype(BF)
        high_ref[:, tile * nodes : (tile + 1) * nodes] = part[half_lanes:].astype(BF)


def node_spectra(slots):
    count, width = slots.shape
    lanes = width // 2
    return pl.pallas_call(
        node_kernel,
        out_shape=(jax.ShapeDtypeStruct((lanes // 2, TILE_DEV * lanes), BF),) * 2,
        in_specs=[pl.BlockSpec(memory_space=pltpu.VMEM)],
        out_specs=(pl.BlockSpec(memory_space=pltpu.VMEM),) * 2,
        scratch_shapes=[pltpu.VMEM((2, count, lanes), F32)],
        compiler_params=pltpu.CompilerParams(vmem_limit_bytes=VMEM_LIMIT),
        cost_estimate=pl.CostEstimate(
            flops=2 * count * lanes * lanes, bytes_accessed=2 << 20, transcendentals=0
        ),
        name="node_spectra",
    )(slots)


def history_kernel(headings, basis_ref, *refs):
    spectra_refs, (out_ref, held_ref, sem) = refs[:-3], refs[-3:]
    count = len(spectra_refs) // 2
    group = basis_ref.shape[1] // count
    half = headings // 2
    pieces = sem.shape[1]
    width = held_ref.shape[2] // pieces
    copies = []
    for heading in range(headings):
        part, inner = divmod(heading, half)
        rows = slice(inner * group, (inner + 1) * group)
        for piece in range(pieces):
            cols = slice(piece * width, (piece + 1) * width)
            chunks = [r[rows, cols] for r in spectra_refs[part * count : (part + 1) * count]]
            spectra = jnp.concatenate(chunks, axis=0)
            held_ref[heading, :, cols] = jnp.dot(
                basis_ref[...], spectra, preferred_element_type=F32
            ).astype(BF)
            window = pl.ds(piece * width, width)
            copy = pltpu.make_async_copy(
                held_ref.at[heading, :, window],
                out_ref.at[heading, :, window],
                sem.at[heading, piece],
            )
            copy.start()
            copies.append(copy)
    for copy in copies:
        copy.wait()


def histories(basis, chunks, headings):
    steps = basis.shape[0]
    nodes = chunks[0].shape[1]
    return pl.pallas_call(
        functools.partial(history_kernel, headings),
        out_shape=jax.ShapeDtypeStruct((headings, steps, nodes), BF),
        in_specs=[pl.BlockSpec(memory_space=pltpu.VMEM)] * (1 + len(chunks)),
        out_specs=pl.BlockSpec(memory_space=pl.ANY),
        scratch_shapes=[
            pltpu.VMEM((headings, steps, nodes), BF),
            pltpu.SemaphoreType.DMA((headings, 2)),
        ],
        compiler_params=pltpu.CompilerParams(vmem_limit_bytes=VMEM_LIMIT),
        cost_estimate=pl.CostEstimate(
            flops=2 * steps * basis.shape[1] * headings * nodes,
            bytes_accessed=6 << 20, transcendentals=0,
        ),
        name="histories",
    )(basis, *chunks)


def window_basis(sources, window, window_len, groups, fl_count):
    source = jnp.repeat(sources, groups)
    group = jnp.tile(jnp.arange(groups, dtype=jnp.int32), sources.shape[0])
    freq_bin = 1 + BIN_STEP * (fl_count * group + source % fl_count)
    step_ids = window * window_len + jnp.arange(window_len, dtype=jnp.int32)
    turn_count = freq_bin[None, :] * step_ids[:, None] % TSTEPS
    turn_angle = turn_count.astype(F32) * (2.0 * math.pi / TSTEPS)
    is_re = (source < fl_count)[None, :]
    return jnp.where(is_re, jnp.cos(turn_angle), -jnp.sin(turn_angle)).astype(BF)


def shards(pressure, spectrum_amp, phase_code, panel_tile, patch_weight):
    owners = lax.axis_size("freq")
    windows = lax.axis_size("node")
    group = lax.axis_index("freq")
    window = lax.axis_index("node")
    _, fl_count, headings, panels = pressure.shape
    width = panels // owners
    capacity = 12
    scaled = scale_spectra(pressure, spectrum_amp, phase_code, group, owners)
    spectra = lax.all_to_all(
        scaled.reshape(owners * windows, headings, width), ("freq", "node"), 0, 0, tiled=True
    ).reshape(owners, windows, headings, width)

    tile_ids = panel_tile.reshape(windows, width)
    weights = patch_weight.reshape(windows * width, 128)
    slot_weight, rank, hot = gather_weights(tile_ids, weights, owners, capacity)
    offsets = [0]
    for step in range(1, windows // 2):
        offsets += [-step, step]
    sources = (window + jnp.asarray(offsets + [windows // 2], jnp.int32)) % windows
    basis = window_basis(sources, window, TSTEPS // windows, owners, fl_count)
    rank, basis = lax.optimization_barrier((rank, basis))

    sent = gather_rows(hot, rank, slot_weight, spectra)
    got = lax.all_to_all(sent, "freq", 0, 0, tiled=True)
    low, high = node_spectra(got.reshape(-1, got.shape[-1]))

    def shift(chunk, distance):
        pairs = [(k, (k + distance) % windows) for k in range(windows)]
        return lax.ppermute(chunk, "node", pairs)

    lows, highs = [low], [high]
    low_up = low_down = low
    high_up = high_down = high
    for step in range(1, windows // 2):
        low_up = shift(low_up, 1)
        high_down = shift(high_down, -1)
        high_up = shift(high_up, 1)
        low_down = shift(low_down, -1)
        lows += [low_up, low_down]
        highs += [high_up, high_down]
    chunks = lows + [shift(low_up, 1)] + highs + [shift(high_down, -1)]
    return histories(basis, chunks, headings)


def solution(mesh):
    placed = (
        P(None, "freq", None, "node"),
        P(),
        P(),
        P("freq", None, None, None),
        P("freq", None, None, None),
    )
    return jax.shard_map(
        shards, mesh=mesh, in_specs=placed, out_specs=P(None, "node", "freq"), check_vma=False
    )
```

```python
import functools
import math

import jax
import jax.numpy as jnp
from jax import lax
from jax.experimental import pallas as pl
from jax.experimental.pallas import tpu as pltpu
from jax.sharding import PartitionSpec as P

F = 128
TSTEPS = 4096
BIN_STEP = 15
PHASE_LEVELS = 4096
TILE_DEV = 8
BF = jnp.bfloat16
F32 = jnp.float32
VMEM_LIMIT = 20 << 20


def scale_kernel(
    group_ref, pressure_hbm, amp_hbm, code_hbm, out_hbm,
    pressure_ref, amp_ref, code_ref, held_ref, table_sem, in_sem, out_sem,
):
    owners, width = held_ref.shape[1], held_ref.shape[3]
    fl_count = pressure_ref.shape[1]
    tables = [
        pltpu.make_async_copy(amp_hbm, amp_ref, table_sem.at[0]),
        pltpu.make_async_copy(code_hbm, code_ref, table_sem.at[1]),
    ]
    arriving = [
        pltpu.make_async_copy(pressure_hbm.at[:, fl], pressure_ref.at[:, fl], in_sem.at[fl])
        for fl in range(fl_count)
    ]
    for copy in tables + arriving:
        copy.start()
    for copy in tables:
        copy.wait()
    lane = lax.broadcasted_iota(jnp.int32, amp_ref.shape, 1)
    angle = code_ref[...].astype(F32) * (2.0 * math.pi / PHASE_LEVELS)
    cosine, sine = jnp.cos(angle), jnp.sin(angle)
    amp = amp_ref[...]
    leaving = []
    for fl in range(fl_count):
        chosen = lane == group_ref[0] * fl_count + fl

        def pick(table):
            return jnp.sum(jnp.where(chosen, table, 0.0), axis=1, keepdims=True)

        a, c, s = pick(amp), pick(cosine), pick(sine)
        arriving[fl].wait()
        for g in range(owners):
            cols = pl.ds(g * width, width)
            re = pressure_ref[0, fl, :, cols].astype(F32)
            im = pressure_ref[1, fl, :, cols].astype(F32)
            held_ref[fl, g] = (a * (re * c - im * s)).astype(BF)
            held_ref[fl_count + fl, g] = (a * (re * s + im * c)).astype(BF)
        for row in (fl, fl_count + fl):
            copy = pltpu.make_async_copy(held_ref.at[row], out_hbm.at[row], out_sem.at[row])
            copy.start()
            leaving.append(copy)
    for copy in leaving:
        copy.wait()


def scale_spectra(pressure, spectrum_amp, phase_code, group, owners):
    parts, fl_count, headings, panels = pressure.shape
    shape = (parts * fl_count, owners, headings, panels // owners)
    return pl.pallas_call(
        scale_kernel,
        out_shape=jax.ShapeDtypeStruct(shape, BF),
        in_specs=[pl.BlockSpec(memory_space=pltpu.SMEM)]
        + [pl.BlockSpec(memory_space=pltpu.HBM)] * 3,
        out_specs=pl.BlockSpec(memory_space=pl.ANY),
        scratch_shapes=[
            pltpu.VMEM(pressure.shape, BF),
            pltpu.VMEM(spectrum_amp.shape, F32),
            pltpu.VMEM(phase_code.shape, jnp.int32),
            pltpu.VMEM(shape, BF),
            pltpu.SemaphoreType.DMA((2,)),
            pltpu.SemaphoreType.DMA((fl_count,)),
            pltpu.SemaphoreType.DMA((parts * fl_count,)),
        ],
        cost_estimate=pl.CostEstimate(flops=2_000_000, bytes_accessed=1 << 20, transcendentals=0),
        name="scale",
    )(group.reshape(1), pressure, spectrum_amp, phase_code)


def fill_tilehot(tile_ref, hot_ref, tile_count):
    blocks, width = tile_ref.shape
    tile_iota = lax.broadcasted_iota(jnp.int32, (tile_count, width), 0)
    for k in range(blocks):
        hot = tile_iota == tile_ref[k : k + 1, :]
        hot_ref[:, k * width : (k + 1) * width] = jnp.where(hot, 1.0, 0.0).astype(BF)


def gather_slots(hot_ref, rank_ref, source_ref, out_ref):
    blocks, width = rank_ref.shape
    owners, capacity, tiles, lanes = out_ref.shape

    def one(s, carry):
        total = jnp.zeros((owners * tiles, lanes), F32)
        for k in range(blocks):
            cols = slice(k * width, (k + 1) * width)
            live = jnp.where(rank_ref[k : k + 1, :] == s.astype(F32), 1.0, 0.0).astype(BF)
            total += jnp.dot(
                hot_ref[:, cols] * live, source_ref[cols, :], preferred_element_type=F32
            )
        out_ref[:, pl.ds(s, 1)] = total.astype(BF).reshape(owners, 1, tiles, lanes)
        return carry

    lax.fori_loop(0, capacity, one, 0)


def weight_kernel(tile_ref, weight_ref, out_ref, rank_ref, hot_ref):
    owners, _, tiles, _ = out_ref.shape
    blocks, width = tile_ref.shape
    fill_tilehot(tile_ref, hot_ref, owners * tiles)
    before = (
        lax.broadcasted_iota(jnp.int32, (width, width), 0)
        < lax.broadcasted_iota(jnp.int32, (width, width), 1)
    )
    before = jnp.where(before, 1.0, 0.0).astype(BF)
    seen = jnp.zeros((owners * tiles, 1), F32)
    for k in range(blocks):
        hot = hot_ref[:, k * width : (k + 1) * width]
        hot32 = hot.astype(F32)
        earlier = jnp.dot(hot, before, preferred_element_type=F32) + seen
        rank_ref[k : k + 1, :] = jnp.sum(hot32 * earlier, axis=0, keepdims=True)
        seen = seen + jnp.sum(hot32, axis=1, keepdims=True)
    gather_slots(hot_ref, rank_ref, weight_ref, out_ref)


def gather_weights(tile_ids, weights, owners, capacity):
    blocks, width = tile_ids.shape
    lanes = weights.shape[1]
    return pl.pallas_call(
        weight_kernel,
        out_shape=(
            jax.ShapeDtypeStruct((owners, capacity, TILE_DEV, lanes), BF),
            jax.ShapeDtypeStruct((blocks, width), F32),
            jax.ShapeDtypeStruct((owners * TILE_DEV, blocks * width), BF),
        ),
        in_specs=[pl.BlockSpec(memory_space=pltpu.VMEM)] * 2,
        out_specs=(pl.BlockSpec(memory_space=pltpu.VMEM),) * 3,
        compiler_params=pltpu.CompilerParams(vmem_limit_bytes=VMEM_LIMIT),
        cost_estimate=pl.CostEstimate(
            flops=2 * owners * capacity * TILE_DEV * blocks * width * lanes,
            bytes_accessed=2 << 20, transcendentals=0,
        ),
        name="weight_slots",
    )(tile_ids, weights)


def row_kernel(hot_ref, rank_ref, weight_ref, spectra_ref, out_ref, rows_ref, packed_ref, masked_ref):
    blocks, groups, headings, width = spectra_ref.shape
    owners, capacity, tiles, _ = out_ref.shape
    lanes = groups * headings
    parts = width // 128
    out_ref[:, :, :, lanes:] = weight_ref[...]
    for k in range(blocks):
        for part in range(parts):
            slot = k * parts + part
            for g in range(groups):
                rows_ref[slot, pl.ds(g, headings, stride=groups), :] = (
                    spectra_ref[k, g, :, part * 128 : (part + 1) * 128].astype(F32)
                )
            packed_ref[:, slot * 128 : (slot + 1) * 128] = rows_ref[slot].astype(BF)

    for step in range(capacity // 2):
        for k in range(blocks):
            cols = slice(k * width, (k + 1) * width)
            rank, rows = rank_ref[k : k + 1, :], packed_ref[:, cols]
            for i in range(2):
                live = jnp.where(rank == float(2 * step + i), 1.0, 0.0).astype(BF)
                masked_ref[i * lanes : (i + 1) * lanes, cols] = rows * live
        total = lax.dot_general(
            hot_ref[...], masked_ref[...], (((1,), (1,)), ((), ())), preferred_element_type=F32
        )
        for i in range(2):
            out_ref[:, 2 * step + i, :, :lanes] = (
                total[:, i * lanes : (i + 1) * lanes].astype(BF).reshape(owners, tiles, lanes)
            )


def gather_rows(hot, rank, weights, spectra):
    blocks, width = rank.shape
    _, groups, headings, _ = spectra.shape
    owners, capacity, tiles, nodes = weights.shape
    lanes = groups * headings
    return pl.pallas_call(
        row_kernel,
        out_shape=pltpu.VMEM((owners, capacity, tiles, lanes + nodes), BF),
        in_specs=[pl.BlockSpec(memory_space=pltpu.VMEM)] * 4,
        out_specs=pl.BlockSpec(memory_space=pltpu.VMEM),
        scratch_shapes=[
            pltpu.VMEM((blocks * width // 128, lanes, 128), F32),
            pltpu.VMEM((lanes, blocks * width), BF),
            pltpu.VMEM((2 * lanes, blocks * width), BF),
        ],
        compiler_params=pltpu.CompilerParams(vmem_limit_bytes=VMEM_LIMIT),
        cost_estimate=pl.CostEstimate(
            flops=2 * owners * capacity * tiles * blocks * width * lanes,
            bytes_accessed=3 << 20, transcendentals=0,
        ),
        name="row_slots",
    )(hot, rank, weights, spectra)


def node_kernel(slots_ref, low_ref, high_ref, wide_ref):
    count, width = slots_ref.shape
    half_lanes = low_ref.shape[0]
    lanes = 2 * half_lanes
    nodes = width - lanes
    for half in range(2):
        wide_ref[half] = slots_ref[:, half * lanes : (half + 1) * lanes].astype(F32)
    for tile in range(TILE_DEV):
        own = pl.ds(tile, count // TILE_DEV, stride=TILE_DEV)
        part = lax.dot_general(
            wide_ref[0, own, :].astype(BF), wide_ref[1, own, :].astype(BF),
            (((0,), (0,)), ((), ())), preferred_element_type=F32,
        )
        low_ref[:, tile * nodes : (tile + 1) * nodes] = part[:half_lanes].astype(BF)
        high_ref[:, tile * nodes : (tile + 1) * nodes] = part[half_lanes:].astype(BF)


def node_spectra(slots):
    count, width = slots.shape
    lanes = width // 2
    return pl.pallas_call(
        node_kernel,
        out_shape=(jax.ShapeDtypeStruct((lanes // 2, TILE_DEV * lanes), BF),) * 2,
        in_specs=[pl.BlockSpec(memory_space=pltpu.VMEM)],
        out_specs=(pl.BlockSpec(memory_space=pltpu.VMEM),) * 2,
        scratch_shapes=[pltpu.VMEM((2, count, lanes), F32)],
        compiler_params=pltpu.CompilerParams(vmem_limit_bytes=VMEM_LIMIT),
        cost_estimate=pl.CostEstimate(
            flops=2 * count * lanes * lanes, bytes_accessed=2 << 20, transcendentals=0
        ),
        name="node_spectra",
    )(slots)


def history_kernel(headings, basis_ref, *refs):
    spectra_refs, (out_ref, held_ref, sem) = refs[:-3], refs[-3:]
    count = len(spectra_refs) // 2
    group = basis_ref.shape[1] // count
    half = headings // 2
    pieces = sem.shape[1]
    width = held_ref.shape[2] // pieces
    copies = []
    for heading in range(headings):
        part, inner = divmod(heading, half)
        rows = slice(inner * group, (inner + 1) * group)
        for piece in range(pieces):
            cols = slice(piece * width, (piece + 1) * width)
            chunks = [r[rows, cols] for r in spectra_refs[part * count : (part + 1) * count]]
            spectra = jnp.concatenate(chunks, axis=0)
            held_ref[heading, :, cols] = jnp.dot(
                basis_ref[...], spectra, preferred_element_type=F32
            ).astype(BF)
            window = pl.ds(piece * width, width)
            copy = pltpu.make_async_copy(
                held_ref.at[heading, :, window],
                out_ref.at[heading, :, window],
                sem.at[heading, piece],
            )
            copy.start()
            copies.append(copy)
    for copy in copies:
        copy.wait()


def histories(basis, chunks, headings):
    steps = basis.shape[0]
    nodes = chunks[0].shape[1]
    return pl.pallas_call(
        functools.partial(history_kernel, headings),
        out_shape=jax.ShapeDtypeStruct((headings, steps, nodes), BF),
        in_specs=[pl.BlockSpec(memory_space=pltpu.VMEM)] * (1 + len(chunks)),
        out_specs=pl.BlockSpec(memory_space=pl.ANY),
        scratch_shapes=[
            pltpu.VMEM((headings, steps, nodes), BF),
            pltpu.SemaphoreType.DMA((headings, 2)),
        ],
        compiler_params=pltpu.CompilerParams(vmem_limit_bytes=VMEM_LIMIT),
        cost_estimate=pl.CostEstimate(
            flops=2 * steps * basis.shape[1] * headings * nodes,
            bytes_accessed=6 << 20, transcendentals=0,
        ),
        name="histories",
    )(basis, *chunks)


def window_basis(sources, window, window_len, groups, fl_count):
    source = jnp.repeat(sources, groups)
    group = jnp.tile(jnp.arange(groups, dtype=jnp.int32), sources.shape[0])
    freq_bin = 1 + BIN_STEP * (fl_count * group + source % fl_count)
    step_ids = window * window_len + jnp.arange(window_len, dtype=jnp.int32)
    turn_count = freq_bin[None, :] * step_ids[:, None] % TSTEPS
    turn_angle = turn_count.astype(F32) * (2.0 * math.pi / TSTEPS)
    is_re = (source < fl_count)[None, :]
    return jnp.where(is_re, jnp.cos(turn_angle), -jnp.sin(turn_angle)).astype(BF)


def shards(pressure, spectrum_amp, phase_code, panel_tile, patch_weight):
    owners = lax.axis_size("freq")
    windows = lax.axis_size("node")
    group = lax.axis_index("freq")
    window = lax.axis_index("node")
    _, fl_count, headings, panels = pressure.shape
    width = panels // owners
    capacity = 12
    scaled = scale_spectra(pressure, spectrum_amp, phase_code, group, owners)
    spectra = lax.all_to_all(
        scaled.reshape(windows * owners, headings, width), ("node", "freq"), 0, 0, tiled=True
    ).reshape(windows, owners, headings, width)

    tile_ids = panel_tile.reshape(windows, width)
    weights = patch_weight.reshape(windows * width, 128)
    slot_weight, rank, hot = gather_weights(tile_ids, weights, owners, capacity)
    offsets = [0]
    for step in range(1, windows // 2):
        offsets += [-step, step]
    sources = (window + jnp.asarray(offsets + [windows // 2], jnp.int32)) % windows
    basis = window_basis(sources, window, TSTEPS // windows, owners, fl_count)
    rank, basis = lax.optimization_barrier((rank, basis))

    sent = gather_rows(hot, rank, slot_weight, spectra)
    got = lax.all_to_all(sent, "freq", 0, 0, tiled=True)
    low, high = node_spectra(got.reshape(-1, got.shape[-1]))

    def shift(chunk, distance):
        pairs = [(k, (k + distance) % windows) for k in range(windows)]
        return lax.ppermute(chunk, "node", pairs)

    lows, highs = [low], [high]
    low_up = low_down = low
    high_up = high_down = high
    for step in range(1, windows // 2):
        low_up = shift(low_up, 1)
        high_down = shift(high_down, -1)
        high_up = shift(high_up, 1)
        low_down = shift(low_down, -1)
        lows += [low_up, low_down]
        highs += [high_up, high_down]
    chunks = lows + [shift(low_up, 1)] + highs + [shift(high_down, -1)]
    return histories(basis, chunks, headings)


def solution(mesh):
    placed = (
        P(None, "freq", None, "node"),
        P(),
        P(),
        P("freq", None, None, None),
        P("freq", None, None, None),
    )
    return jax.shard_map(
        shards, mesh=mesh, in_specs=placed, out_specs=P(None, "node", "freq"), check_vma=False
    )
```
